32 devices in a mesh: row: 4 (over z), col: 8 (over y, x, core).
Axes of the slice: x: 2, y: 2, z: 4, core: 2. Of those that a mesh axis runs over, the one named last changes fastest.
Arguments:
- rhs_window: float32 [4, 4096, 256], P(None, 'row'), may hold values from -6 to 6
- rhs_below: float32 [32768, 256], P(('row', 'col')), may hold values from -6 to 6
- dinv: bfloat16 [4, 4096, 4096], P(None, 'col', 'row'), as said below
- couple: bfloat16 [6, 4096, 4096], P(None, 'row', 'col'), may hold values from -0.0546875 to 0.0546875
- window_mask: int32 [6, 32], P(None, 'row'), may hold values 0 or 1
- below_factor: bfloat16 [4, 32768, 4096], P(None, 'row', 'col'), may hold values from -0.0625 to 0.0625
- below_mask: int32 [4, 256], P(None, 'row'), may hold values 0 or 1
Outputs:
- solution: float32 [4, 4096, 256], P(None, 'col')
- below_rhs: float32 [32768, 256], P(('row', 'col'))
The draws below stay inside these ranges and needn't reach their ends.
Inputs may be any that keep to these rules, and one draw needn't show every extreme that they name: Each block of dinv is lower triangular with a positive diagonal.
All inputs are finite; a program needn't handle non-finite values. No bound on the sum of `window_mask` or of `below_mask` on one device may be relied on, other than what follows from the above.
Results may differ from the reference program's by a relative error of at most 0.0065.
Values sent between devices are 32-bit elements; how exact they have to be, the bound alone decides.
No kernel may reach another device: no remote copies, remote signals or barrier semaphores. Data moves between devices by JAX's collectives and lax.ppermute only.
A program may use at most 128 MiB of HBM per device.

```python
import math
import jax
import jax.numpy as jnp
from jax import lax

SNW = 4096
NRHS = 256
BLK = 128
PANELS = 4
PAIRS = 6
BELOW = 32768


def draw_dinv(key, part):
    first_key, second_key = jax.random.split(jax.random.fold_in(key, 17))
    shape = (PANELS, SNW, SNW)
    row_ids = lax.broadcasted_iota(jnp.int32, shape, 1)
    col_ids = lax.broadcasted_iota(jnp.int32, shape, 2)
    noise = jax.random.normal(second_key, shape, jnp.float32) * (0.8 / math.sqrt(SNW))
    diag_vals = jax.random.uniform(first_key, shape, jnp.float32, 0.6, 1.4)
    lower = jnp.where(col_ids < row_ids, noise, jnp.zeros(shape, jnp.float32))
    result = jnp.where(row_ids == col_ids, diag_vals, lower)
    return result.astype(jnp.bfloat16)


def set_ends(array, key, low, largest):
    longest = array.shape.index(max(array.shape))
    spots = []
    for shift in (0, 1):
        where = [jax.random.randint(jax.random.fold_in(key, axis), (), 0, length) for axis, length in enumerate(array.shape)]
        where[longest] = (where[longest] + shift) % array.shape[longest]
        spots.append(tuple(where))
    return array.at[spots[0]].set(low).at[spots[1]].set(largest)


def strengthened(values, stream_key, source, target, blocks, factor):
    owner, partner = [(jnp.arange(values.shape[axis_at]) // (values.shape[axis_at] // blocks)).reshape([-1 if axis == axis_at else 1 for axis in range(values.ndim)]) for axis_at in (source, target)]
    chosen = jax.random.permutation(stream_key, blocks)[partner]
    strong = (owner == chosen) | (owner == (partner + blocks // 2) % blocks)
    return jnp.where(strong, factor * values, values)


def shard_levels(rng, shape, pieces, least, high):
    loudness = 1.0
    for position, blocks in pieces:
        steps = jax.random.uniform(jax.random.fold_in(jax.random.fold_in(rng, 6), position), (blocks,), jnp.float32, least / len(pieces), high / len(pieces))
        loudness = loudness * jnp.repeat(jnp.exp(steps), shape[position] // blocks).reshape((-1,) + (1,) * (len(shape) - 1 - position))
    return loudness


def scatter_about(key, dims, deviation, most, shards=(), dtype=jnp.bfloat16):
    gain = shard_levels(key, dims, shards, -0.22, 0.18) if shards else 1.0
    drawn = jax.random.normal(key, dims, jnp.float32) * deviation * gain
    return jnp.minimum(jnp.maximum(drawn, -most), most).astype(dtype)


def gaussian_with(own_key, extent, spread, bound, cuts, heavy, dtype=jnp.bfloat16):
    array = spread * jax.random.normal(own_key, extent, jnp.float32)
    if cuts:
        array = array * shard_levels(own_key, extent, cuts, -0.22, 0.18)
    return jnp.clip(strengthened(array, jax.random.fold_in(own_key, 3), *heavy), -bound, bound).astype(dtype)


def setup_inputs(seed: int = 0) -> dict:
    key_of = jax.random.split(jax.random.key(seed), 8)
    return {
        "rhs_window": scatter_about(key_of[0], (PANELS, SNW, NRHS), 1.0, 6.0, ((1, 4),), jnp.float32),
        "rhs_below": scatter_about(key_of[1], (BELOW, NRHS), 1.0, 6.0, ((0, 32),), jnp.float32),
        "dinv": draw_dinv(jax.random.fold_in(key_of[7], 71), 0),
        "couple": scatter_about(key_of[3], (PAIRS, SNW, SNW), (3 * SNW) ** -0.5, 0.0546875, ((1, 4), (2, 8))),
        "window_mask": set_ends((jax.random.randint(key_of[4], (PAIRS, SNW // BLK), 0, 4) < 3).astype(jnp.int32), jax.random.fold_in(key_of[4], 1), 0, 1),
        "below_factor": gaussian_with(key_of[5], (PANELS, BELOW, SNW), (PANELS * SNW) ** -0.5, 0.0625, ((1, 4), (2, 8)), (2, 1, 8, 2.0)),
        "below_mask": set_ends((jax.random.randint(key_of[6], (PANELS, BELOW // BLK), 0, 4) < 3).astype(jnp.int32), jax.random.fold_in(key_of[6], 1), 0, 1),
    }


def reference(rhs_window, rhs_below, dinv, couple, window_mask, below_factor, below_mask):
    window_gain = jnp.repeat(window_mask.astype(jnp.float32), BLK, axis=1)
    below_gain = jnp.repeat(below_mask.astype(jnp.float32), BLK, axis=1)
    solutions = []
    solved_bf = []
    for target in range(PANELS):
        partial_value = jnp.zeros((SNW, NRHS), jnp.float32)
        for source in range(target):
            pair_index = target * (target - 1) // 2 + source
            product = jnp.dot(couple[pair_index], solved_bf[source], preferred_element_type=jnp.float32)
            partial_value = partial_value + window_gain[pair_index][:, None] * product
        reduced = (rhs_window[target] - partial_value).astype(jnp.bfloat16)
        solved = jnp.dot(dinv[target], reduced, preferred_element_type=jnp.float32)
        solutions.append(solved)
        solved_bf.append(solved.astype(jnp.bfloat16))
    below_sum = jnp.zeros((BELOW, NRHS), jnp.float32)
    for panel in range(PANELS):
        product = jnp.dot(below_factor[panel], solved_bf[panel], preferred_element_type=jnp.float32)
        below_sum = below_sum + below_gain[panel][:, None] * product
    return jnp.stack(solutions), rhs_below - below_sum
```

```python
import functools

import jax
import jax.numpy as jnp
from jax import lax
from jax.experimental import pallas as pl
from jax.experimental.pallas import tpu as pltpu
from jax.sharding import PartitionSpec as P

BLK = 128
PANELS = 4
F32 = jnp.float32


def swap(x, axis, mask):
    n = lax.axis_size(axis)
    return lax.ppermute(x, axis, [(i, i ^ mask) for i in range(n)])


def sum_parts(parts, axis, masks):
    parts = list(parts)
    for step in range(len(masks)):
        got = [swap(p, axis, masks[(step + j) % len(masks)]) for j, p in enumerate(parts)]
        parts = [p + g for p, g in zip(parts, got)]
    return parts


def halves(x):
    rows = x.shape[0] // 2
    return [x[:rows], x[rows:]]


def sum_rest(x, axis, masks):
    return jnp.concatenate(sum_parts(halves(x), axis, masks), axis=0)


def sum_paired(x, axis, masks):
    bit = lax.axis_index(axis) & 1
    rows = x.shape[0] // 2
    mine = lax.dynamic_slice_in_dim(x, bit * rows, rows, 0)
    other = lax.dynamic_slice_in_dim(x, (1 - bit) * rows, rows, 0)
    total = sum_rest(mine + swap(other, axis, 1), axis, masks)
    back = swap(total, axis, 1)
    low = jnp.where(bit == 0, total, back)
    high = jnp.where(bit == 0, back, total)
    return jnp.concatenate([low, high], axis=0)


def sum_row(x):
    n = lax.axis_size("row")
    return sum_rest(x, "row", (1, 3)) if n == 4 else sum_paired(x, "row", (2, 6))


def sum_col(x):
    n = lax.axis_size("col")
    return sum_paired(x, "col", tuple(2 << b for b in range(n.bit_length() - 2)))


def early_kernel(mask, f_ref, x_ref, o_ref):
    tile = o_ref.shape[0]
    base = pl.program_id(0) * (tile // BLK)
    for sub in range(tile // BLK):
        rows = pl.ds(sub * BLK, BLK)
        total = None
        for p in range(PANELS - 1):
            part = jnp.dot(f_ref[p, rows, :], x_ref[p], preferred_element_type=F32)
            part = part * mask[p, base + sub].astype(F32)
            total = part if total is None else total + part
        o_ref[rows, :] = total


def early_below(mask, factor, solved):
    _, rows, depth = factor.shape
    cols = solved.shape[-1]
    tile = min(1024, rows)
    return pl.pallas_call(
        early_kernel,
        out_shape=jax.ShapeDtypeStruct((rows, cols), F32),
        grid_spec=pltpu.PrefetchScalarGridSpec(
            num_scalar_prefetch=1,
            grid=(rows // tile,),
            in_specs=[
                pl.BlockSpec((PANELS - 1, tile, depth), lambda i, m: (0, i, 0)),
                pl.BlockSpec((PANELS - 1, depth, cols), lambda i, m: (0, 0, 0)),
            ],
            out_specs=pl.BlockSpec((tile, cols), lambda i, m: (i, 0)),
        ),
        cost_estimate=pl.CostEstimate(
            flops=2 * 3 * rows * depth * cols,
            bytes_accessed=6 * rows * depth + 4 * rows * cols,
            transcendentals=0,
        ),
        name="early_below",
    )(mask, factor, solved)


def last_kernel(part, mask, sel, f_ref, x_ref, a_ref, o_ref):
    tile = o_ref.shape[0]
    block = (2 * pl.program_id(0) + sel[0]) * 2 + part
    base = block * (tile // BLK)
    for sub in range(tile // BLK):
        rows = pl.ds(sub * BLK, BLK)
        term = jnp.dot(f_ref[0, rows, :], x_ref[...], preferred_element_type=F32)
        o_ref[rows, :] = a_ref[rows, :] + term * mask[PANELS - 1, base + sub].astype(F32)


def last_below(part, mask, sel, factor, solved, early, n):
    _, rows, depth = factor.shape
    cols = solved.shape[-1]
    tile = rows // n // 2

    def at(i, m, s):
        return (2 * i + s[0]) * 2 + part

    return pl.pallas_call(
        functools.partial(last_kernel, part),
        out_shape=jax.ShapeDtypeStruct((rows // 4, cols), F32),
        grid_spec=pltpu.PrefetchScalarGridSpec(
            num_scalar_prefetch=2,
            grid=(n // 2,),
            in_specs=[
                pl.BlockSpec((1, tile, depth), lambda i, m, s: (PANELS - 1, at(i, m, s), 0)),
                pl.BlockSpec((depth, cols), lambda i, m, s: (0, 0)),
                pl.BlockSpec((tile, cols), lambda i, m, s: (at(i, m, s), 0)),
            ],
            out_specs=pl.BlockSpec((tile, cols), lambda i, m, s: (i, 0)),
        ),
        cost_estimate=pl.CostEstimate(
            flops=rows * depth * cols // 2,
            bytes_accessed=rows * depth // 2 + 2 * rows * cols,
            transcendentals=0,
        ),
        name="last_below",
    )(mask, sel, factor, solved, early)


def scatter_rest(kept, order):
    me = lax.axis_index("col")
    left = list(range(kept.ndim - 2, 0, -1))
    for bit in order:
        dim = left.index(bit)
        mine = (me >> bit) & 1
        send = lax.dynamic_index_in_dim(kept, 1 - mine, dim, keepdims=False)
        keep = lax.dynamic_index_in_dim(kept, mine, dim, keepdims=False)
        left.remove(bit)
        kept = keep + swap(send, "col", 1 << bit)
    return kept


def local(rhs_window, rhs_below, dinv, couple, window_mask, below_factor, below_mask):
    window_gain = jnp.repeat(window_mask.astype(F32), BLK, axis=1)
    n = lax.axis_size("col")
    bits = n.bit_length() - 1
    me = lax.axis_index("col")
    solutions, solved = [], []
    for target in range(PANELS):
        right = rhs_window[target]
        if target > 0:
            partial = None
            for source in range(target):
                pair = target * (target - 1) // 2 + source
                product = jnp.dot(couple[pair], solved[source], preferred_element_type=F32)
                product = window_gain[pair][:, None] * product
                partial = product if partial is None else partial + product
            right = right - sum_col(partial)
        reduced = right.astype(jnp.bfloat16)
        total = sum_row(jnp.dot(dinv[target], reduced, preferred_element_type=F32))
        solutions.append(total)
        solved.append(total.astype(jnp.bfloat16))
    early = early_below(below_mask, below_factor, jnp.stack(solved[:-1]))
    mine = (me & 1).astype(jnp.int32)[None]
    sends = [
        swap(last_below(j, below_mask, 1 - mine, below_factor, solved[-1], early, n), "col", 1)
        for j in range(2)
    ]
    keeps = [last_below(j, below_mask, mine, below_factor, solved[-1], early, n) for j in range(2)]
    done = []
    for j in range(2):
        kept = keeps[j] + sends[j]
        kept = kept.reshape((2,) * (bits - 1) + (-1, kept.shape[-1]))
        order = list(range(1, bits))
        done.append(scatter_rest(kept, order[j:] + order[:j]))
    return (jnp.stack(solutions), rhs_below - jnp.concatenate(done, axis=0))


def solution(mesh):
    return jax.shard_map(
        local,
        mesh=mesh,
        in_specs=(
            P(None, "row", None),
            P(("row", "col"), None),
            P(None, "col", "row"),
            P(None, "row", "col"),
            P(None, "row"),
            P(None, "row", "col"),
            P(None, "row"),
        ),
        out_specs=(P(None, "col", None), P(("row", "col"), None)),
        check_vma=False,
    )
```

```python
import functools

import jax
import jax.numpy as jnp
from jax import lax
from jax.experimental import pallas as pl
from jax.experimental.pallas import tpu as pltpu
from jax.sharding import PartitionSpec as P

BLK = 128
PANELS = 4
F32 = jnp.float32
BF16 = jnp.bfloat16
VMEM = pl.BlockSpec(memory_space=pltpu.VMEM)
SMEM = pl.BlockSpec(memory_space=pltpu.SMEM)
HBM = pl.BlockSpec(memory_space=pltpu.HBM)


def swap(x, axis, mask):
    n = lax.axis_size(axis)
    return lax.ppermute(x, axis, [(i, i ^ mask) for i in range(n)])


def after(x, *others):
    return lax.optimization_barrier((x, *others))[0]


def half(x, bit, dim):
    size = x.shape[dim] // 2
    return lax.dynamic_slice_in_dim(x, bit * size, size, dim)


def halves(x):
    rows = x.shape[0] // 2
    return [x[:rows], x[rows:]]


def sum_parts(parts, axis, masks, queue):
    for step in range(len(masks)):
        got = [swap(p, axis, masks[(step + j) % len(masks)]) for j, p in enumerate(parts)]
        new = [p + g for p, g in zip(parts, got)]
        if queue:
            new = lax.optimization_barrier((*new, queue.pop(0)(parts[-1])))[: len(new)]
        parts = list(new)
    return parts


def sum_row(parts, queue):
    if lax.axis_size("row") == 4:
        return sum_parts(parts, "row", (1, 3), queue)
    bit = lax.axis_index("row") & 1
    x = jnp.concatenate(parts, axis=0)
    mine = half(x, bit, 0) + swap(half(x, 1 - bit, 0), "row", 1)
    mine = jnp.concatenate(sum_parts(halves(mine), "row", (2, 6), queue), axis=0)
    back = swap(mine, "row", 1)
    return [jnp.where(bit == 0, mine, back), jnp.where(bit == 0, back, mine)]


def col_masks():
    n = lax.axis_size("col")
    return tuple(2 << b for b in range(n.bit_length() - 2))


def stage_kernel(sel, c_ref, d_ref, *refs):
    outs, sem = refs[:4], refs[4]
    copies = []
    for side in range(2):
        half_of = sel[0] if side else 1 - sel[0]
        rows, depth = outs[side].shape[1], outs[2 + side].shape[2]
        sources = (c_ref.at[:, pl.ds(half_of * rows, rows), :], d_ref.at[:, :, pl.ds(half_of * depth, depth)])
        for k, source in enumerate(sources):
            copies.append(pltpu.make_async_copy(source, outs[2 * k + side], sem.at[2 * k + side]))
    for copy in copies:
        copy.start()
    for copy in copies:
        copy.wait()


def stage(bit, couple, dinv):
    pairs, rows, depth = couple.shape
    panels, height, width = dinv.shape
    shapes = [(pairs, rows // 2, depth)] * 2 + [(panels, height, width // 2)] * 2
    out = pl.pallas_call(
        stage_kernel,
        out_shape=[jax.ShapeDtypeStruct(shape, BF16) for shape in shapes],
        in_specs=[SMEM, HBM, HBM],
        out_specs=[VMEM] * 4,
        scratch_shapes=[pltpu.SemaphoreType.DMA((4,))],
        compiler_params=pltpu.CompilerParams(vmem_limit_bytes=44 << 20),
        name="stage",
    )(bit, couple, dinv)
    return out[:2], out[2:]


def last_kernel(base, *refs):
    f_ref, outs, sem = refs[0], refs[1:-1], refs[-1]
    own = outs[0].shape[0]
    copies = []
    for q, out in enumerate(outs):
        source = f_ref.at[PANELS - 1, pl.ds(base[q] * own, own), :]
        copies.append(pltpu.make_async_copy(source, out, sem.at[q]))
    for copy in copies:
        copy.start()
    for copy in copies:
        copy.wait()


def last_rows(blocks, factor, own):
    _, rows, depth = factor.shape
    n = rows // own
    return pl.pallas_call(
        last_kernel,
        out_shape=[jax.ShapeDtypeStruct((own, depth), BF16)] * n,
        in_specs=[SMEM, HBM],
        out_specs=[VMEM] * n,
        scratch_shapes=[pltpu.SemaphoreType.DMA((n,))],
        compiler_params=pltpu.CompilerParams(vmem_limit_bytes=33 << 20),
        name="last_rows",
    )(blocks, factor)


def scatter(sums, part, bits):
    order = list(range(1, bits))
    order = order[-part:] + order[:-part] if part else order
    for bit in order:
        mask = 1 << bit
        got = {q: swap(x, "col", mask) for q, x in sorted(sums.items(), reverse=True) if q & mask}
        sums = {q: x + got[q | mask] for q, x in sums.items() if not q & mask}
    return sums[0]


def local(rhs_window, rhs_below, dinv, couple, window_mask, below_factor, below_mask):
    n = lax.axis_size("col")
    bits = n.bit_length() - 1
    me = lax.axis_index("col")
    bit = me & 1
    sel = bit.astype(jnp.int32)[None]
    sides = (1 - bit, bit)
    blocks = me ^ jnp.arange(n, dtype=jnp.int32)
    gain = jnp.repeat(window_mask.astype(F32), BLK, axis=1)
    gains = [half(gain, s, 1) for s in sides]
    rhs = [[halves(half(r, s, 0)) for s in sides] for r in rhs_window]
    own = rhs_below.shape[0]
    rows = below_factor.shape[1] // 2
    below_gain = jnp.repeat(below_mask.astype(F32), BLK, axis=1)
    early = [None, None]
    store = {}

    def early_step(panel, top, solved, dep):
        factor = below_factor[panel, top * rows : (top + 1) * rows]
        term = jnp.dot(factor, after(solved, dep), preferred_element_type=F32)
        term = below_gain[panel, top * rows : (top + 1) * rows, None] * term
        early[top] = early[top] + term if panel else term
        return early[top]

    def stage_step(dep):
        store["couple"], store["dinv"] = stage(after(sel, dep), couple, dinv)
        return store["couple"][0]

    def last_step(dep):
        store["last"] = last_rows(after(blocks, dep), below_factor, own)
        return store["last"][0]

    def tail(q, solved):
        term = jnp.dot(store["last"][q], solved, preferred_element_type=F32)
        scale = lax.dynamic_slice_in_dim(below_gain[-1], (me ^ q) * own, own, 0)
        at = ((me ^ q) % (n // 2)) * own
        parts = [lax.dynamic_slice_in_dim(e, at, own, 0) for e in early]
        base = jnp.where((me ^ q) < n // 2, parts[0], parts[1])
        return base + scale[:, None] * term

    def update(target, side, solved):
        total = None
        for source in range(target):
            pair = target * (target - 1) // 2 + source
            product = jnp.dot(store["couple"][side][pair], solved[source], preferred_element_type=F32)
            product = gains[side][pair][:, None] * product
            total = product if total is None else total + product
        return total

    solutions, solved = [], []
    queue = [stage_step, last_step]
    for target in range(PANELS):
        right = rhs[target]
        if target > 0:
            away = swap(update(target, 0, solved), "col", 1)
            home = sum_parts(halves(update(target, 1, solved) + away), "col", col_masks(), [])
            back = [swap(h, "col", 1) for h in home]
            right = [[r - b for r, b in zip(rhs[target][0], back)], [r - h for r, h in zip(rhs[target][1], home)]]
        parts = []
        for piece in range(2):
            total = None
            for side in (1, 0):
                if target == 0:
                    inverse = half(dinv[0], sides[side], 1)
                else:
                    inverse = store["dinv"][side][target]
                height, width = inverse.shape[0] // 2, inverse.shape[1] // 2
                for k in range(2):
                    block = inverse[piece * height : (piece + 1) * height, k * width : (k + 1) * width]
                    product = jnp.dot(block, right[side][k].astype(BF16), preferred_element_type=F32)
                    total = product if total is None else total + product
            parts.append(total)
        parts = sum_row(parts, queue)
        while queue:
            queue.pop(0)(parts[0])
        solutions.append(jnp.concatenate(parts, axis=0))
        solved.append(jnp.concatenate([p.astype(BF16) for p in parts], axis=0))
        if target < PANELS - 1:
            queue = [functools.partial(early_step, target, top, solved[-1]) for top in range(2)]
    sent = {q: swap(tail(q, solved[-1]), "col", 1) for q in range(n - 1, 0, -2)}
    sums = {q: halves(tail(q, solved[-1]) + sent[q + 1]) for q in range(n - 2, -1, -2)}
    done = [scatter({q: x[j] for q, x in sums.items()}, j, bits) for j in range(2)]
    return (jnp.stack(solutions), rhs_below - jnp.concatenate(done, axis=0))


def solution(mesh):
    return jax.shard_map(
        local,
        mesh=mesh,
        in_specs=(
            P(None, "row", None),
            P(("row", "col"), None),
            P(None, "col", "row"),
            P(None, "row", "col"),
            P(None, "row"),
            P(None, "row", "col"),
            P(None, "row"),
        ),
        out_specs=(P(None, "col", None), P(("row", "col"), None)),
        check_vma=False,
    )
```

```python
import functools

import jax
import jax.numpy as jnp
from jax import lax
from jax.experimental import pallas as pl
from jax.experimental.layout import Layout, with_layout_constraint
from jax.experimental.pallas import tpu as pltpu
from jax.sharding import PartitionSpec as P

BLK = 128
PANELS = 4
F32 = jnp.float32
BF16 = jnp.bfloat16
VMEM = pl.BlockSpec(memory_space=pltpu.VMEM)
SMEM = pl.BlockSpec(memory_space=pltpu.SMEM)
HBM = pl.BlockSpec(memory_space=pltpu.HBM)


def swap(x, axis, mask):
    n = lax.axis_size(axis)
    return lax.ppermute(x, axis, [(i, i ^ mask) for i in range(n)])


def after(x, *others):
    return lax.optimization_barrier((x, *others))[0]


def half(x, bit, dim):
    size = x.shape[dim] // 2
    return lax.dynamic_slice_in_dim(x, bit * size, size, dim)


def halves(x):
    rows = x.shape[0] // 2
    return [x[:rows], x[rows:]]


def sum_parts(parts, axis, masks, queue):
    for step in range(len(masks)):
        got = [swap(p, axis, masks[(step + j) % len(masks)]) for j, p in enumerate(parts)]
        new = [p + g for p, g in zip(parts, got)]
        if queue:
            new = lax.optimization_barrier((*new, queue.pop(0)(parts[-1])))[: len(new)]
        parts = list(new)
    return parts


def sum_row(parts, queue):
    if lax.axis_size("row") == 4:
        return sum_parts(parts, "row", (1, 2), queue)
    bit = lax.axis_index("row") & 1
    x = jnp.concatenate(parts, axis=0)
    mine = half(x, bit, 0) + swap(half(x, 1 - bit, 0), "row", 1)
    mine = jnp.concatenate(sum_parts(halves(mine), "row", (2, 6), queue), axis=0)
    back = swap(mine, "row", 1)
    return [jnp.where(bit == 0, mine, back), jnp.where(bit == 0, back, mine)]


def col_masks():
    n = lax.axis_size("col")
    return tuple(2 << b for b in range(n.bit_length() - 2))


def stage_kernel(sel, c_ref, d_ref, *refs):
    outs, sem = refs[:4], refs[4]
    copies = []
    for side in range(2):
        half_of = sel[0] if side else 1 - sel[0]
        rows, depth = outs[side].shape[1], outs[2 + side].shape[2]
        sources = (c_ref.at[:, pl.ds(half_of * rows, rows), :], d_ref.at[:, :, pl.ds(half_of * depth, depth)])
        for k, source in enumerate(sources):
            copies.append(pltpu.make_async_copy(source, outs[2 * k + side], sem.at[2 * k + side]))
    for copy in copies:
        copy.start()
    for copy in copies:
        copy.wait()


def stage(bit, couple, dinv):
    pairs, rows, depth = couple.shape
    panels, height, width = dinv.shape
    shapes = [(pairs, rows // 2, depth)] * 2 + [(panels, height, width // 2)] * 2
    out = pl.pallas_call(
        stage_kernel,
        out_shape=[jax.ShapeDtypeStruct(shape, BF16) for shape in shapes],
        in_specs=[SMEM, HBM, HBM],
        out_specs=[VMEM] * 4,
        scratch_shapes=[pltpu.SemaphoreType.DMA((4,))],
        compiler_params=pltpu.CompilerParams(vmem_limit_bytes=44 << 20),
        name="stage",
    )(bit, couple, dinv)
    return out[:2], out[2:]


def row_major(x):
    return with_layout_constraint(x, Layout(major_to_minor=tuple(range(x.ndim))))


def last_kernel(base, *refs):
    f_ref, outs, sem = refs[0], refs[1:-1], refs[-1]
    own = outs[0].shape[0]
    copies = []
    for q, out in enumerate(outs):
        source = f_ref.at[PANELS - 1, pl.ds(base[q] * own, own), :]
        copies.append(pltpu.make_async_copy(source, out, sem.at[q]))
    for copy in copies:
        copy.start()
    for copy in copies:
        copy.wait()


def last_rows(blocks, factor, own):
    _, rows, depth = factor.shape
    n = rows // own
    return pl.pallas_call(
        last_kernel,
        out_shape=[jax.ShapeDtypeStruct((own, depth), BF16)] * n,
        in_specs=[SMEM, HBM],
        out_specs=[VMEM] * n,
        scratch_shapes=[pltpu.SemaphoreType.DMA((n,))],
        compiler_params=pltpu.CompilerParams(vmem_limit_bytes=33 << 20),
        name="last_rows",
    )(blocks, factor)


def scatter(sums, part, bits):
    order = list(range(1, bits))
    order = order[-part:] + order[:-part] if part else order
    for bit in order:
        mask = 1 << bit
        got = {q: swap(x, "col", mask) for q, x in sorted(sums.items(), reverse=True) if q & mask}
        sums = {q: x + got[q | mask] for q, x in sums.items() if not q & mask}
    return sums[0]


def local(rhs_window, rhs_below, dinv, couple, window_mask, below_factor, below_mask):
    n = lax.axis_size("col")
    bits = n.bit_length() - 1
    me = lax.axis_index("col")
    bit = me & 1
    sel = bit.astype(jnp.int32)[None]
    sides = (1 - bit, bit)
    blocks = me ^ jnp.arange(n, dtype=jnp.int32)
    gain = jnp.repeat(window_mask.astype(F32), BLK, axis=1)
    gains = [half(gain, s, 1) for s in sides]
    rhs = [None] + [[halves(half(rhs_window[t], s, 0)) for s in sides] for t in range(1, PANELS)]
    own = rhs_below.shape[0]
    rows = below_factor.shape[1] // 2
    below_gain = jnp.repeat(below_mask.astype(F32), BLK, axis=1)
    early = [None, None]
    store = {}

    def early_step(panel, top, solved, dep):
        factor = below_factor[panel, top * rows : (top + 1) * rows]
        term = jnp.dot(factor, after(solved, dep), preferred_element_type=F32)
        term = below_gain[panel, top * rows : (top + 1) * rows, None] * term
        early[top] = row_major(early[top] + term if panel else term)
        return early[top]

    def stage_step(dep):
        store["couple"], store["dinv"] = stage(after(sel, dep), couple, dinv)
        return store["couple"][0]

    def last_step(dep):
        store["last"] = last_rows(after(blocks, dep), below_factor, own)
        gain_of = after(below_gain[-1], dep)
        scales = [lax.dynamic_slice_in_dim(gain_of, (me ^ q) * own, own, 0) for q in range(n)]
        store["scale"] = lax.optimization_barrier(tuple(scales))
        return store["scale"][0]

    def tail(q, solved):
        term = jnp.dot(store["last"][q], solved, preferred_element_type=F32)
        scale = store["scale"][q]
        at = ((me ^ q) % (n // 2)) * own
        parts = [lax.dynamic_slice_in_dim(e, at, own, 0) for e in early]
        base = jnp.where((me ^ q) < n // 2, parts[0], parts[1])
        return row_major(base + scale[:, None] * term)

    def update(target, side, solved):
        total = None
        for source in range(target):
            pair = target * (target - 1) // 2 + source
            product = jnp.dot(store["couple"][side][pair], solved[source], preferred_element_type=F32)
            product = gains[side][pair][:, None] * product
            total = product if total is None else total + product
        return total

    solutions, solved = [], []
    queue = [stage_step, last_step]
    for target in range(PANELS):
        right = rhs[target]
        if target > 0:
            away = swap(update(target, 0, solved), "col", 1)
            home = sum_parts(halves(update(target, 1, solved) + away), "col", col_masks(), [])
            back = [swap(h, "col", 1) for h in home]
            right = [[r - b for r, b in zip(rhs[target][0], back)], [r - h for r, h in zip(rhs[target][1], home)]]
        parts = []
        if target == 0:
            reduced = rhs_window[0].astype(BF16)
            parts = [jnp.dot(d, reduced, preferred_element_type=F32) for d in halves(dinv[0])]
        for piece in range(2 if target else 0):
            total = None
            for side in (1, 0):
                inverse = store["dinv"][side][target]
                height, width = inverse.shape[0] // 2, inverse.shape[1] // 2
                for k in range(2):
                    block = inverse[piece * height : (piece + 1) * height, k * width : (k + 1) * width]
                    product = jnp.dot(block, right[side][k].astype(BF16), preferred_element_type=F32)
                    total = product if total is None else total + product
            parts.append(total)
        parts = sum_row(parts, queue)
        while queue:
            queue.pop(0)(parts[0])
        solutions.append(jnp.concatenate(parts, axis=0))
        solved.append(jnp.concatenate([p.astype(BF16) for p in parts], axis=0))
        if target < PANELS - 1:
            queue = [functools.partial(early_step, target, top, solved[-1]) for top in range(2)]
    sent = {q: swap(tail(q, solved[-1]), "col", 1) for q in range(n - 1, 0, -2)}
    sums = {q: halves(tail(q, solved[-1]) + sent[q + 1]) for q in range(n - 2, -1, -2)}
    sums = {q: lax.optimization_barrier(tuple(x)) for q, x in sums.items()}
    done = [scatter({q: x[j] for q, x in sums.items()}, j, bits) for j in range(2)]
    below = [r - d for r, d in zip(halves(rhs_below), done)]
    return (jnp.stack(solutions), jnp.concatenate(below, axis=0))


def solution(mesh):
    return jax.shard_map(
        local,
        mesh=mesh,
        in_specs=(
            P(None, "row", None),
            P(("row", "col"), None),
            P(None, "col", "row"),
            P(None, "row", "col"),
            P(None, "row"),
            P(None, "row", "col"),
            P(None, "row"),
        ),
        out_specs=(P(None, "col", None), P(("row", "col"), None)),
        check_vma=False,
    )
```

```python
import functools

import jax
import jax.numpy as jnp
from jax import lax
from jax.experimental import pallas as pl
from jax.experimental.layout import Layout, with_layout_constraint
from jax.experimental.pallas import tpu as pltpu
from jax.sharding import PartitionSpec as P

BLK = 128
PANELS = 4
F32 = jnp.float32
BF16 = jnp.bfloat16
VMEM = pl.BlockSpec(memory_space=pltpu.VMEM)
SMEM = pl.BlockSpec(memory_space=pltpu.SMEM)
HBM = pl.BlockSpec(memory_space=pltpu.HBM)


def swap(x, axis, mask):
    n = lax.axis_size(axis)
    return lax.ppermute(x, axis, [(i, i ^ mask) for i in range(n)])


def after(x, *others):
    return lax.optimization_barrier((x, *others))[0]


def half(x, bit, dim):
    size = x.shape[dim] // 2
    return lax.dynamic_slice_in_dim(x, bit * size, size, dim)


def halves(x):
    rows = x.shape[0] // 2
    return [x[:rows], x[rows:]]


def sum_parts(parts, axis, masks, queue):
    for step in range(len(masks)):
        got = [swap(p, axis, masks[(step + j) % len(masks)]) for j, p in enumerate(parts)]
        new = [p + g for p, g in zip(parts, got)]
        if queue:
            new = lax.optimization_barrier((*new, queue.pop(0)(parts[-1])))[: len(new)]
        parts = list(new)
    return parts


def exchange(parts, axis, masks, step):
    return [swap(p, axis, masks[(step + j) % len(masks)]) for j, p in enumerate(parts)]


def sum_row(parts, queue):
    if lax.axis_size("row") == 4:
        return sum_parts(parts, "row", (1, 2), queue)
    bit = lax.axis_index("row") & 1
    x = jnp.concatenate(parts, axis=0)
    mine = half(x, bit, 0) + swap(half(x, 1 - bit, 0), "row", 1)
    mine = jnp.concatenate(sum_parts(halves(mine), "row", (2, 6), queue), axis=0)
    back = swap(mine, "row", 1)
    return [jnp.where(bit == 0, mine, back), jnp.where(bit == 0, back, mine)]


def col_masks():
    n = lax.axis_size("col")
    return tuple(2 << b for b in range(n.bit_length() - 2))


def stage_kernel(sel, c_ref, d_ref, *refs):
    outs, sem = refs[:4], refs[4]
    copies = []
    for side in range(2):
        half_of = sel[0] if side else 1 - sel[0]
        rows, depth = outs[side].shape[1], outs[2 + side].shape[2]
        sources = (c_ref.at[:, pl.ds(half_of * rows, rows), :], d_ref.at[:, :, pl.ds(half_of * depth, depth)])
        for k, source in enumerate(sources):
            copies.append(pltpu.make_async_copy(source, outs[2 * k + side], sem.at[2 * k + side]))
    for copy in copies:
        copy.start()
    for copy in copies:
        copy.wait()


def stage(bit, couple, dinv):
    pairs, rows, depth = couple.shape
    panels, height, width = dinv.shape
    shapes = [(pairs, rows // 2, depth)] * 2 + [(panels, height, width // 2)] * 2
    out = pl.pallas_call(
        stage_kernel,
        out_shape=[jax.ShapeDtypeStruct(shape, BF16) for shape in shapes],
        in_specs=[SMEM, HBM, HBM],
        out_specs=[VMEM] * 4,
        scratch_shapes=[pltpu.SemaphoreType.DMA((4,))],
        compiler_params=pltpu.CompilerParams(vmem_limit_bytes=44 << 20),
        name="stage",
    )(bit, couple, dinv)
    return out[:2], out[2:]


def row_major(x):
    return with_layout_constraint(x, Layout(major_to_minor=tuple(range(x.ndim))))


def last_kernel(base, *refs):
    f_ref, outs, sem = refs[0], refs[1:-1], refs[-1]
    own = outs[0].shape[0]
    copies = []
    for q, out in enumerate(outs):
        source = f_ref.at[PANELS - 1, pl.ds(base[q] * own, own), :]
        copies.append(pltpu.make_async_copy(source, out, sem.at[q]))
    for copy in copies:
        copy.start()
    for copy in copies:
        copy.wait()


def last_rows(blocks, factor, own):
    _, rows, depth = factor.shape
    n = rows // own
    return pl.pallas_call(
        last_kernel,
        out_shape=[jax.ShapeDtypeStruct((own, depth), BF16)] * n,
        in_specs=[SMEM, HBM],
        out_specs=[VMEM] * n,
        scratch_shapes=[pltpu.SemaphoreType.DMA((n,))],
        compiler_params=pltpu.CompilerParams(vmem_limit_bytes=33 << 20),
        name="last_rows",
    )(blocks, factor)


def scatter(sums, part, bits):
    order = list(range(1, bits))
    order = order[-part:] + order[:-part] if part else order
    for bit in order:
        mask = 1 << bit
        got = {q: swap(x, "col", mask) for q, x in sorted(sums.items(), reverse=True) if q & mask}
        sums = {q: x + got[q | mask] for q, x in sums.items() if not q & mask}
    return sums[0]


def local(rhs_window, rhs_below, dinv, couple, window_mask, below_factor, below_mask):
    n = lax.axis_size("col")
    bits = n.bit_length() - 1
    me = lax.axis_index("col")
    bit = me & 1
    sel = bit.astype(jnp.int32)[None]
    sides = (1 - bit, bit)
    blocks = me ^ jnp.arange(n, dtype=jnp.int32)
    gain = jnp.repeat(window_mask.astype(F32), BLK, axis=1)
    gains = [half(gain, s, 1) for s in sides]
    rhs = [None] + [[halves(half(rhs_window[t], s, 0)) for s in sides] for t in range(1, PANELS)]
    own = rhs_below.shape[0]
    rows = below_factor.shape[1] // 2
    below_gain = jnp.repeat(below_mask.astype(F32), BLK, axis=1)
    early = [None, None]
    store = {}

    def early_step(panel, top, solved, dep):
        factor = below_factor[panel, top * rows : (top + 1) * rows]
        term = jnp.dot(factor, after(solved, dep), preferred_element_type=F32)
        term = below_gain[panel, top * rows : (top + 1) * rows, None] * term
        early[top] = row_major(early[top] + term if panel else term)
        return early[top]

    def stage_step(dep):
        store["couple"], store["dinv"] = stage(after(sel, dep), couple, dinv)
        return store["couple"][0]

    def last_step(dep):
        store["last"] = last_rows(after(blocks, dep), below_factor, own)
        gain_of = after(below_gain[-1], dep)
        scales = [lax.dynamic_slice_in_dim(gain_of, (me ^ q) * own, own, 0) for q in range(n)]
        store["scale"] = lax.optimization_barrier(tuple(scales))
        return store["scale"][0]

    def tail(q, piece, solved):
        cols = solved.shape[1]
        term = jnp.dot(store["last"][q], solved, preferred_element_type=F32)
        at = ((me ^ q) % (n // 2)) * own
        parts = [lax.dynamic_slice(e, (at, piece * cols), (own, cols)) for e in early]
        base = jnp.where((me ^ q) < n // 2, parts[0], parts[1])
        return row_major(base + store["scale"][q][:, None] * term)

    def tail_pairs(piece, solved):
        sent = {q: swap(tail(q, piece, solved), "col", 1) for q in range(n - 1, 0, -2)}
        sums = {q: halves(tail(q, piece, solved) + sent[q + 1]) for q in range(n - 2, -1, -2)}
        return {q: lax.optimization_barrier(tuple(x)) for q, x in sums.items()}

    def tail_rest(sums):
        return [scatter({q: x[j] for q, x in sums.items()}, j, bits) for j in range(2)]

    def inverse_dots(target, right):
        parts = []
        for piece in range(2):
            total = None
            for side in (1, 0):
                inverse = store["dinv"][side][target]
                height, width = inverse.shape[0] // 2, inverse.shape[1] // 2
                for k in range(2):
                    block = inverse[piece * height : (piece + 1) * height, k * width : (k + 1) * width]
                    product = jnp.dot(block, right[side][k].astype(BF16), preferred_element_type=F32)
                    total = product if total is None else total + product
            parts.append(total)
        return parts

    def update(target, side, solved):
        total = None
        for source in range(target):
            pair = target * (target - 1) // 2 + source
            product = jnp.dot(store["couple"][side][pair], solved[source], preferred_element_type=F32)
            product = gains[side][pair][:, None] * product
            total = product if total is None else total + product
        return total

    solutions, solved = [], []
    queue = [stage_step, last_step]
    for target in range(PANELS):
        right = rhs[target]
        if target > 0:
            away = swap(update(target, 0, solved), "col", 1)
            home = sum_parts(halves(update(target, 1, solved) + away), "col", col_masks(), [])
            back = [swap(h, "col", 1) for h in home]
            right = [[r - b for r, b in zip(rhs[target][0], back)], [r - h for r, h in zip(rhs[target][1], home)]]
        if target == PANELS - 1:
            break
        if target == 0:
            reduced = rhs_window[0].astype(BF16)
            parts = [jnp.dot(d, reduced, preferred_element_type=F32) for d in halves(dinv[0])]
        else:
            parts = inverse_dots(target, right)
        parts = sum_row(parts, queue)
        while queue:
            queue.pop(0)(parts[0])
        solutions.append(jnp.concatenate(parts, axis=0))
        solved.append(jnp.concatenate([p.astype(BF16) for p in parts], axis=0))
        queue = [functools.partial(early_step, target, top, solved[-1]) for top in range(2)]
    cols = rhs_window.shape[-1] // 2
    first, second = [
        inverse_dots(target, [[r[:, k * cols : (k + 1) * cols] for r in side] for side in right]) for k in range(2)
    ]

    def joined(parts):
        return jnp.concatenate([p.astype(BF16) for p in parts], axis=0)

    if lax.axis_size("row") == 4:
        masks = (1, 2)
        got = exchange(first, "row", masks, 0)
        done = queue[0](first[-1])
        first = lax.optimization_barrier((*[p + g for p, g in zip(first, got)], done))[:2]
        got = exchange(first, "row", masks, 1)
        second = lax.optimization_barrier((*second, *first))[:2]
        other = exchange(second, "row", masks, 0)
        done = queue[1](second[-1])
        first = lax.optimization_barrier((*[p + g for p, g in zip(first, got)], done))[:2]
        second = lax.optimization_barrier((*[p + g for p, g in zip(second, other)], *first))[:2]
        got = exchange(second, "row", masks, 1)
        sums = tail_pairs(0, after(joined(first), *second))
        ready = [x for q in sums if q for x in sums[q]]
        second = lax.optimization_barrier((*[p + g for p, g in zip(second, got)], *ready))[:2]
    else:
        first = sum_row(first, queue)
        second = sum_row(second, queue)
        sums = tail_pairs(0, joined(first))
    later = tail_pairs(1, joined(second))
    done = [tail_rest(sums), tail_rest(later)]
    solutions = [after(x, later[n - 2][0]) for x in solutions]
    solutions.append(jnp.concatenate([jnp.concatenate(p, axis=1) for p in zip(first, second)], axis=0))
    below = [r - jnp.concatenate(d, axis=1) for r, d in zip(halves(rhs_below), zip(*done))]
    return (jnp.stack(solutions), jnp.concatenate(below, axis=0))


def solution(mesh):
    return jax.shard_map(
        local,
        mesh=mesh,
        in_specs=(
            P(None, "row", None),
            P(("row", "col"), None),
            P(None, "col", "row"),
            P(None, "row", "col"),
            P(None, "row"),
            P(None, "row", "col"),
            P(None, "row"),
        ),
        out_specs=(P(None, "col", None), P(("row", "col"), None)),
        check_vma=False,
    )
```

```python
import functools

import jax
import jax.numpy as jnp
from jax import lax
from jax.experimental import pallas as pl
from jax.experimental.layout import Layout, with_layout_constraint
from jax.experimental.pallas import tpu as pltpu
from jax.sharding import PartitionSpec as P

BLK = 128
PANELS = 4
F32 = jnp.float32
BF16 = jnp.bfloat16
VMEM = pl.BlockSpec(memory_space=pltpu.VMEM)
SMEM = pl.BlockSpec(memory_space=pltpu.SMEM)
HBM = pl.BlockSpec(memory_space=pltpu.HBM)


def swap(x, axis, mask):
    n = lax.axis_size(axis)
    return lax.ppermute(x, axis, [(i, i ^ mask) for i in range(n)])


def after(x, *others):
    return lax.optimization_barrier((x, *others))[0]


def half(x, bit, dim):
    size = x.shape[dim] // 2
    return lax.dynamic_slice_in_dim(x, bit * size, size, dim)


def halves(x):
    rows = x.shape[0] // 2
    return [x[:rows], x[rows:]]


def sum_parts(parts, axis, masks, queue):
    for step in range(len(masks)):
        got = [swap(p, axis, masks[(step + j) % len(masks)]) for j, p in enumerate(parts)]
        new = [p + g for p, g in zip(parts, got)]
        if queue:
            new = lax.optimization_barrier((*new, queue.pop(0)(parts[-1])))[: len(new)]
        parts = list(new)
    return parts


def exchange(parts, axis, masks, step):
    return [swap(p, axis, masks[(step + j) % len(masks)]) for j, p in enumerate(parts)]


def sum_row(parts, queue):
    if lax.axis_size("row") == 4:
        return sum_parts(parts, "row", (1, 2), queue)
    bit = lax.axis_index("row") & 1
    x = jnp.concatenate(parts, axis=0)
    mine = half(x, bit, 0) + swap(half(x, 1 - bit, 0), "row", 1)
    mine = jnp.concatenate(sum_parts(halves(mine), "row", (2, 6), queue), axis=0)
    back = swap(mine, "row", 1)
    return [jnp.where(bit == 0, mine, back), jnp.where(bit == 0, back, mine)]


def col_masks():
    n = lax.axis_size("col")
    return tuple(2 << b for b in range(n.bit_length() - 2))


def stage_kernel(dim, sel, x_ref, *refs):
    outs, sem = refs[:2], refs[2]
    size = outs[0].shape[dim]
    copies = []
    for side in range(2):
        half_of = sel[0] if side else 1 - sel[0]
        at = [slice(None)] * 3
        at[dim] = pl.ds(half_of * size, size)
        copies.append(pltpu.make_async_copy(x_ref.at[tuple(at)], outs[side], sem.at[side]))
    for copy in copies:
        copy.start()
    for copy in copies:
        copy.wait()


def stage(sel, x, dim):
    shape = list(x.shape)
    shape[dim] //= 2
    return pl.pallas_call(
        functools.partial(stage_kernel, dim),
        out_shape=[jax.ShapeDtypeStruct(shape, BF16)] * 2,
        in_specs=[SMEM, HBM],
        out_specs=[VMEM] * 2,
        scratch_shapes=[pltpu.SemaphoreType.DMA((2,))],
        compiler_params=pltpu.CompilerParams(vmem_limit_bytes=44 << 20),
        name="stage",
    )(sel, x)


def row_major(x):
    return with_layout_constraint(x, Layout(major_to_minor=tuple(range(x.ndim))))


def last_kernel(base, *refs):
    f_ref, outs, sem = refs[0], refs[1:-1], refs[-1]
    own = outs[0].shape[0]
    copies = []
    for q, out in enumerate(outs):
        source = f_ref.at[PANELS - 1, pl.ds(base[q] * own, own), :]
        copies.append(pltpu.make_async_copy(source, out, sem.at[q]))
    for copy in copies:
        copy.start()
    for copy in copies:
        copy.wait()


def last_rows(blocks, factor, own):
    _, rows, depth = factor.shape
    n = rows // own
    return pl.pallas_call(
        last_kernel,
        out_shape=[jax.ShapeDtypeStruct((own, depth), BF16)] * n,
        in_specs=[SMEM, HBM],
        out_specs=[VMEM] * n,
        scratch_shapes=[pltpu.SemaphoreType.DMA((n,))],
        compiler_params=pltpu.CompilerParams(vmem_limit_bytes=33 << 20),
        name="last_rows",
    )(blocks, factor)


def scatter(sums, part, bits):
    order = list(range(1, bits))
    order = order[-part:] + order[:-part] if part else order
    for bit in order:
        mask = 1 << bit
        got = {q: swap(x, "col", mask) for q, x in sorted(sums.items(), reverse=True) if q & mask}
        sums = {q: x + got[q | mask] for q, x in sums.items() if not q & mask}
    return sums[0]


def local(rhs_window, rhs_below, dinv, couple, window_mask, below_factor, below_mask):
    n = lax.axis_size("col")
    bits = n.bit_length() - 1
    me = lax.axis_index("col")
    bit = me & 1
    sel = bit.astype(jnp.int32)[None]
    sides = (1 - bit, bit)
    blocks = me ^ jnp.arange(n, dtype=jnp.int32)
    gain = jnp.repeat(window_mask.astype(F32), BLK, axis=1)
    gains = [half(gain, s, 1) for s in sides]
    rhs = [None] + [[halves(half(rhs_window[t], s, 0)) for s in sides] for t in range(1, PANELS)]
    own = rhs_below.shape[0]
    rows = below_factor.shape[1] // 2
    below_gain = jnp.repeat(below_mask.astype(F32), BLK, axis=1)
    early = [None, None]
    store = {}

    def early_step(panel, top, solved, dep):
        factor = below_factor[panel, top * rows : (top + 1) * rows]
        term = jnp.dot(factor, after(solved, dep), preferred_element_type=F32)
        term = below_gain[panel, top * rows : (top + 1) * rows, None] * term
        early[top] = row_major(early[top] + term if panel else term)
        return early[top]

    def couple_step(dep):
        store["couple"] = stage(after(sel, dep), couple, 1)
        return store["couple"][0]

    def dinv_step(dep):
        store["dinv"] = stage(after(sel, dep), dinv, 2)
        return store["dinv"][0]

    def last_step(dep):
        store["last"] = last_rows(after(blocks, dep), below_factor, own)
        gain_of = after(below_gain[-1], dep)
        scales = [lax.dynamic_slice_in_dim(gain_of, (me ^ q) * own, own, 0) for q in range(n)]
        store["scale"] = lax.optimization_barrier(tuple(scales))
        return store["scale"][0]

    def tail(q, piece, solved):
        cols = solved.shape[1]
        term = jnp.dot(store["last"][q], solved, preferred_element_type=F32)
        at = ((me ^ q) % (n // 2)) * own
        parts = [lax.dynamic_slice(e, (at, piece * cols), (own, cols)) for e in early]
        base = jnp.where((me ^ q) < n // 2, parts[0], parts[1])
        return row_major(base + store["scale"][q][:, None] * term)

    def tail_pairs(piece, solved):
        sent = {q: swap(tail(q, piece, solved), "col", 1) for q in range(n - 1, 0, -2)}
        sums = {q: halves(tail(q, piece, solved) + sent[q + 1]) for q in range(n - 2, -1, -2)}
        return {q: lax.optimization_barrier(tuple(x)) for q, x in sums.items()}

    def tail_rest(sums):
        return [scatter({q: x[j] for q, x in sums.items()}, j, bits) for j in range(2)]

    def inverse_dots(target, right):
        parts = []
        for piece in range(2):
            total = None
            for side in (1, 0):
                inverse = store["dinv"][side][target]
                height, width = inverse.shape[0] // 2, inverse.shape[1] // 2
                for k in range(2):
                    block = inverse[piece * height : (piece + 1) * height, k * width : (k + 1) * width]
                    product = jnp.dot(block, right[side][k].astype(BF16), preferred_element_type=F32)
                    total = product if total is None else total + product
            parts.append(total)
        return parts

    def update(target, side, solved):
        total = None
        for source in range(target):
            pair = target * (target - 1) // 2 + source
            product = jnp.dot(store["couple"][side][pair], solved[source], preferred_element_type=F32)
            product = gains[side][pair][:, None] * product
            total = product if total is None else total + product
        return total

    solutions, solved = [], []
    queue = [dinv_step, couple_step, last_step]
    for target in range(PANELS):
        right = rhs[target]
        if target > 0:
            away = swap(update(target, 0, solved), "col", 1)
            home = sum_parts(halves(update(target, 1, solved) + away), "col", col_masks(), [])
            back = [swap(h, "col", 1) for h in home]
            right = [[r - b for r, b in zip(rhs[target][0], back)], [r - h for r, h in zip(rhs[target][1], home)]]
        if target == PANELS - 1:
            break
        if target == 0:
            reduced = rhs_window[0].astype(BF16)
            parts = [jnp.dot(d, reduced, preferred_element_type=F32) for d in halves(dinv[0])]
        else:
            parts = inverse_dots(target, right)
        parts = sum_row(parts, queue)
        while queue:
            queue.pop(0)(parts[0])
        solutions.append(jnp.concatenate(parts, axis=0))
        solved.append(jnp.concatenate([p.astype(BF16) for p in parts], axis=0))
        queue = [functools.partial(early_step, target, top, solved[-1]) for top in range(2)]
    cols = rhs_window.shape[-1] // 2
    first, second = [
        inverse_dots(target, [[r[:, k * cols : (k + 1) * cols] for r in side] for side in right]) for k in range(2)
    ]

    def joined(parts):
        return jnp.concatenate([p.astype(BF16) for p in parts], axis=0)

    if lax.axis_size("row") == 4:
        masks = (1, 2)
        got = exchange(first, "row", masks, 0)
        done = queue[0](first[-1])
        first = lax.optimization_barrier((*[p + g for p, g in zip(first, got)], done))[:2]
        got = exchange(first, "row", masks, 1)
        second = lax.optimization_barrier((*second, *first))[:2]
        other = exchange(second, "row", masks, 0)
        done = queue[1](second[-1])
        first = lax.optimization_barrier((*[p + g for p, g in zip(first, got)], done))[:2]
        second = lax.optimization_barrier((*[p + g for p, g in zip(second, other)], *first))[:2]
        got = exchange(second, "row", masks, 1)
        sums = tail_pairs(0, after(joined(first), *second))
        ready = [x for q in sums if q for x in sums[q]]
        second = lax.optimization_barrier((*[p + g for p, g in zip(second, got)], *ready))[:2]
    else:
        first = sum_row(first, queue)
        second = sum_row(second, queue)
        sums = tail_pairs(0, joined(first))
    later = tail_pairs(1, joined(second))
    done = [tail_rest(sums), tail_rest(later)]
    solutions = [after(x, later[n - 2][0]) for x in solutions]
    solutions.append(jnp.concatenate([jnp.concatenate(p, axis=1) for p in zip(first, second)], axis=0))
    below = [r - jnp.concatenate(d, axis=1) for r, d in zip(halves(rhs_below), zip(*done))]
    return (jnp.stack(solutions), jnp.concatenate(below, axis=0))


def solution(mesh):
    return jax.shard_map(
        local,
        mesh=mesh,
        in_specs=(
            P(None, "row", None),
            P(("row", "col"), None),
            P(None, "col", "row"),
            P(None, "row", "col"),
            P(None, "row"),
            P(None, "row", "col"),
            P(None, "row"),
        ),
        out_specs=(P(None, "col", None), P(("row", "col"), None)),
        check_vma=False,
    )
```

```python
import functools

import jax
import jax.numpy as jnp
from jax import lax
from jax.experimental import pallas as pl
from jax.experimental.layout import Layout, with_layout_constraint
from jax.experimental.pallas import tpu as pltpu
from jax.sharding import PartitionSpec as P

BLK = 128
PANELS = 4
F32 = jnp.float32
BF16 = jnp.bfloat16
VMEM = pl.BlockSpec(memory_space=pltpu.VMEM)
SMEM = pl.BlockSpec(memory_space=pltpu.SMEM)
HBM = pl.BlockSpec(memory_space=pltpu.HBM)


def swap(x, axis, mask):
    n = lax.axis_size(axis)
    return lax.ppermute(x, axis, [(i, i ^ mask) for i in range(n)])


def after(x, *others):
    return lax.optimization_barrier((x, *others))[0]


def half(x, bit, dim):
    size = x.shape[dim] // 2
    return lax.dynamic_slice_in_dim(x, bit * size, size, dim)


def halves(x):
    rows = x.shape[0] // 2
    return [x[:rows], x[rows:]]


def sum_parts(parts, axis, masks, queue):
    for step in range(len(masks)):
        got = [swap(p, axis, masks[(step + j) % len(masks)]) for j, p in enumerate(parts)]
        new = [p + g for p, g in zip(parts, got)]
        if queue:
            new = lax.optimization_barrier((*new, *jax.tree.leaves(queue.pop(0)(parts[-1]))))[: len(new)]
        parts = list(new)
    return parts


def exchange(parts, axis, masks, step):
    return [swap(p, axis, masks[(step + j) % len(masks)]) for j, p in enumerate(parts)]


def sum_row(parts, queue):
    if lax.axis_size("row") == 4:
        return sum_parts(parts, "row", (1, 2), queue)
    bit = lax.axis_index("row") & 1
    x = jnp.concatenate(parts, axis=0)
    mine = half(x, bit, 0) + swap(half(x, 1 - bit, 0), "row", 1)
    mine = jnp.concatenate(sum_parts(halves(mine), "row", (2, 6), queue), axis=0)
    back = swap(mine, "row", 1)
    return [jnp.where(bit == 0, mine, back), jnp.where(bit == 0, back, mine)]


def col_masks():
    n = lax.axis_size("col")
    return tuple(2 << b for b in range(n.bit_length() - 2))


def stage_kernel(dim, sel, x_ref, *refs):
    outs, sem = refs[:2], refs[2]
    size = outs[0].shape[dim]
    copies = []
    for side in range(2):
        half_of = sel[0] if side else 1 - sel[0]
        at = [slice(None)] * 3
        at[dim] = pl.ds(half_of * size, size)
        copies.append(pltpu.make_async_copy(x_ref.at[tuple(at)], outs[side], sem.at[side]))
    for copy in copies:
        copy.start()
    for copy in copies:
        copy.wait()


def stage(sel, x, dim):
    shape = list(x.shape)
    shape[dim] //= 2
    return pl.pallas_call(
        functools.partial(stage_kernel, dim),
        out_shape=[jax.ShapeDtypeStruct(shape, BF16)] * 2,
        in_specs=[SMEM, HBM],
        out_specs=[VMEM] * 2,
        scratch_shapes=[pltpu.SemaphoreType.DMA((2,))],
        compiler_params=pltpu.CompilerParams(vmem_limit_bytes=44 << 20),
        name="stage",
    )(sel, x)


def row_major(x):
    return with_layout_constraint(x, Layout(major_to_minor=tuple(range(x.ndim))))


def last_kernel(base, *refs):
    f_ref, outs, sem = refs[0], refs[1:-1], refs[-1]
    own = outs[0].shape[0]
    copies = []
    for q, out in enumerate(outs):
        source = f_ref.at[PANELS - 1, pl.ds(base[q] * own, own), :]
        copies.append(pltpu.make_async_copy(source, out, sem.at[q]))
    for copy in copies:
        copy.start()
    for copy in copies:
        copy.wait()


def last_rows(blocks, factor, own):
    _, rows, depth = factor.shape
    n = rows // own
    return pl.pallas_call(
        last_kernel,
        out_shape=[jax.ShapeDtypeStruct((own, depth), BF16)] * n,
        in_specs=[SMEM, HBM],
        out_specs=[VMEM] * n,
        scratch_shapes=[pltpu.SemaphoreType.DMA((n,))],
        compiler_params=pltpu.CompilerParams(vmem_limit_bytes=33 << 20),
        name="last_rows",
    )(blocks, factor)


def scatter(sums, part, bits):
    order = list(range(1, bits))
    order = order[-part:] + order[:-part] if part else order
    for bit in order:
        mask = 1 << bit
        got = {q: swap(x, "col", mask) for q, x in sorted(sums.items(), reverse=True) if q & mask}
        sums = {q: x + got[q | mask] for q, x in sums.items() if not q & mask}
    return sums[0]


def local(rhs_window, rhs_below, dinv, couple, window_mask, below_factor, below_mask):
    n = lax.axis_size("col")
    bits = n.bit_length() - 1
    me = lax.axis_index("col")
    bit = me & 1
    sel = bit.astype(jnp.int32)[None]
    sides = (1 - bit, bit)
    blocks = me ^ jnp.arange(n, dtype=jnp.int32)
    gain = jnp.repeat(window_mask.astype(F32), BLK, axis=1)
    gains = [half(gain, s, 1) for s in sides]
    own = rhs_below.shape[0]
    rows = below_factor.shape[1] // 2
    below_gain = jnp.repeat(below_mask.astype(F32), BLK, axis=1)
    early = [None, None]
    store = {}

    def early_step(panel, top, solved, dep):
        factor = below_factor[panel, top * rows : (top + 1) * rows]
        term = jnp.dot(factor, after(solved, dep), preferred_element_type=F32)
        term = below_gain[panel, top * rows : (top + 1) * rows, None] * term
        early[top] = row_major(early[top] + term if panel else term)
        return early[top]

    def couple_step(dep):
        store["couple"] = stage(after(sel, dep), couple, 1)
        key = after(bit, dep)
        rows_of = rhs_window.shape[1] // 2
        cuts = [
            lax.dynamic_slice(rhs_window, (t, s * rows_of, 0), (1, rows_of, rhs_window.shape[2]))[0]
            for t in range(1, PANELS)
            for s in (1 - key, key)
        ]
        cuts = lax.optimization_barrier(tuple(cuts))
        for t in range(1, PANELS):
            store["rhs", t] = [halves(x) for x in cuts[2 * t - 2 : 2 * t]]
        return (store["couple"][0], *cuts)

    def dinv_step(dep):
        store["dinv"] = stage(after(sel, dep), dinv, 2)
        return store["dinv"][0]

    def last_step(dep):
        store["last"] = last_rows(after(blocks, dep), below_factor, own)
        gain_of = after(below_gain[-1], dep)
        scales = [lax.dynamic_slice_in_dim(gain_of, (me ^ q) * own, own, 0) for q in range(n)]
        store["scale"] = lax.optimization_barrier(tuple(scales))
        return store["scale"][0]

    def tail(q, piece, solved):
        cols = solved.shape[1]
        term = jnp.dot(store["last"][q], solved, preferred_element_type=F32)
        at = ((me ^ q) % (n // 2)) * own
        parts = [lax.dynamic_slice(e, (at, piece * cols), (own, cols)) for e in early]
        base = jnp.where((me ^ q) < n // 2, parts[0], parts[1])
        return row_major(base + store["scale"][q][:, None] * term)

    def tail_pairs(piece, solved):
        sent = {q: swap(tail(q, piece, solved), "col", 1) for q in range(n - 1, 0, -2)}
        sums = {q: halves(tail(q, piece, solved) + sent[q + 1]) for q in range(n - 2, -1, -2)}
        return {q: lax.optimization_barrier(tuple(x)) for q, x in sums.items()}

    def tail_rest(sums):
        return [scatter({q: x[j] for q, x in sums.items()}, j, bits) for j in range(2)]

    def inverse_dots(target, right):
        parts = []
        for piece in range(2):
            total = None
            for side in (1, 0):
                inverse = store["dinv"][side][target]
                height, width = inverse.shape[0] // 2, inverse.shape[1] // 2
                for k in range(2):
                    block = inverse[piece * height : (piece + 1) * height, k * width : (k + 1) * width]
                    product = jnp.dot(block, right[side][k].astype(BF16), preferred_element_type=F32)
                    total = product if total is None else total + product
            parts.append(total)
        return parts

    def update(target, side, solved):
        total = None
        for source in range(target):
            pair = target * (target - 1) // 2 + source
            product = jnp.dot(store["couple"][side][pair], solved[source], preferred_element_type=F32)
            product = gains[side][pair][:, None] * product
            total = product if total is None else total + product
        return total

    solutions, solved = [], []
    queue = [dinv_step, couple_step, last_step]
    for target in range(PANELS):
        rhs = store.get(("rhs", target))
        right = rhs
        if target > 0:
            away = swap(update(target, 0, solved), "col", 1)
            home = sum_parts(halves(update(target, 1, solved) + away), "col", col_masks(), [])
            back = [swap(h, "col", 1) for h in home]
            right = [[r - b for r, b in zip(rhs[0], back)], [r - h for r, h in zip(rhs[1], home)]]
        if target == PANELS - 1:
            break
        if target == 0:
            reduced = rhs_window[0].astype(BF16)
            parts = [jnp.dot(d, reduced, preferred_element_type=F32) for d in halves(dinv[0])]
        else:
            parts = inverse_dots(target, right)
        parts = sum_row(parts, queue)
        while queue:
            queue.pop(0)(parts[0])
        solutions.append(jnp.concatenate(parts, axis=0))
        solved.append(jnp.concatenate([p.astype(BF16) for p in parts], axis=0))
        queue = [functools.partial(early_step, target, top, solved[-1]) for top in range(2)]
    cols = rhs_window.shape[-1] // 2
    first, second = [
        inverse_dots(target, [[r[:, k * cols : (k + 1) * cols] for r in side] for side in right]) for k in range(2)
    ]

    def joined(parts):
        return jnp.concatenate([p.astype(BF16) for p in parts], axis=0)

    if lax.axis_size("row") == 4:
        masks = (1, 2)
        got = exchange(first, "row", masks, 0)
        done = queue[0](first[-1])
        first = lax.optimization_barrier((*[p + g for p, g in zip(first, got)], done))[:2]
        got = exchange(first, "row", masks, 1)
        second = lax.optimization_barrier((*second, *first))[:2]
        other = exchange(second, "row", masks, 0)
        done = queue[1](second[-1])
        first = lax.optimization_barrier((*[p + g for p, g in zip(first, got)], done))[:2]
        second = lax.optimization_barrier((*[p + g for p, g in zip(second, other)], *first))[:2]
        got = exchange(second, "row", masks, 1)
        sums = tail_pairs(0, after(joined(first), *second))
        ready = [x for q in sums if q for x in sums[q]]
        second = lax.optimization_barrier((*[p + g for p, g in zip(second, got)], *ready))[:2]
    else:
        first = sum_row(first, queue)
        second = sum_row(second, queue)
        sums = tail_pairs(0, joined(first))
    later = tail_pairs(1, joined(second))
    done = [tail_rest(sums), tail_rest(later)]
    solutions = [after(x, later[n - 2][0]) for x in solutions]
    solutions.append(jnp.concatenate([jnp.concatenate(p, axis=1) for p in zip(first, second)], axis=0))
    below = [r - jnp.concatenate(d, axis=1) for r, d in zip(halves(rhs_below), zip(*done))]
    return (jnp.stack(solutions), jnp.concatenate(below, axis=0))


def solution(mesh):
    return jax.shard_map(
        local,
        mesh=mesh,
        in_specs=(
            P(None, "row", None),
            P(("row", "col"), None),
            P(None, "col", "row"),
            P(None, "row", "col"),
            P(None, "row"),
            P(None, "row", "col"),
            P(None, "row"),
        ),
        out_specs=(P(None, "col", None), P(("row", "col"), None)),
        check_vma=False,
    )
```
